32 devices in a mesh: section: 2 (over y), dp: 16 (over z, x, core).
Axes of the slice: x: 2, y: 2, z: 4, core: 2. Of those that a mesh axis runs over, the one named last changes fastest.
Arguments:
- inputs: bfloat16 [4096, 768], P('dp'), may hold values from -6 to 6
- cotangent: bfloat16 [4096, 768], P('dp'), may hold values from -6 to 6
- segments: int32 [4096], P('dp'), may hold values from 0 to 3, as said below
- qkv_weight: bfloat16 [2, 768, 2304], P('section', 'dp'), may hold values from -0.21875 to 0.21875
- out_weight: bfloat16 [2, 768, 768], P('section', 'dp'), may hold values from -0.875 to 0.875
- up_weight: bfloat16 [2, 768, 3072], P('section', 'dp'), may hold values from -0.21875 to 0.21875
- down_weight: bfloat16 [2, 3072, 768], P('section', 'dp'), may hold values from -0.109375 to 0.109375
- norm_params: bfloat16 [2, 4, 768], P('section', None, 'dp'), may hold values from 0.5 to 1.5
- bias_params: bfloat16 [2, 4, 768], P('section', None, 'dp'), may hold values from -3 to 3
- up_bias: bfloat16 [2, 3072], P('section', 'dp'), may hold values from -3 to 3
Outputs:
- layer_outputs: bfloat16 [2, 4096, 768], P('section', 'dp')
- input_grads: bfloat16 [2, 4096, 768], P('section', 'dp')
- qkv_grad: float32 [2, 768, 2304], P('section', 'dp')
- out_grad: float32 [2, 768, 768], P('section', 'dp')
- up_grad: float32 [2, 768, 3072], P('section', 'dp')
- down_grad: float32 [2, 3072, 768], P('section', 'dp')
- norm_grad: float32 [2, 4, 768], P('section', None, 'dp')
- bias_grad: float32 [2, 4, 768], P('section', None, 'dp')
- up_bias_grad: float32 [2, 3072], P('section', 'dp')
The draws below stay inside these ranges and needn't reach their ends.
Inputs may be any that keep to these rules, and one draw needn't show every extreme that they name: `segments`: within each aligned block of 128 positions the numbers start at 0 and rise by one where a new sequence starts; every block holds exactly 4 sequences; no sequence crosses a block.
All inputs are finite; a program needn't handle non-finite values.
Results may differ from the reference program's by a relative error of at most 0.014.
Values may be sent and summed in bfloat16 or wider, within the bound.
A program may use at most 256 MiB of HBM per device.

```python
import math
import jax
import jax.numpy as jnp
from jax import lax

D = 768
FF = 3072
HEAD = 64
ROT = 16
SEQS = 4
PACK = 128
TOKENS = 4096


def draw_segments(key, part):
    packs = TOKENS // PACK
    key_rows = jax.random.split(key, packs)
    chosen = jax.vmap(lambda one: jax.random.permutation(one, PACK - 1)[:SEQS - 1] + 1)(key_rows)
    index = jnp.arange(PACK, dtype=jnp.int32)
    starts = jnp.any(index[None, None, :] == chosen[:, :, None], axis=1)
    ids = jnp.cumsum(starts.astype(jnp.int32), axis=1)
    return ids.reshape(TOKENS).astype(jnp.int32)


def block_levels(rng, extent, cuts, smallest, high):
    factor_of, own = 1.0, jax.random.fold_in(rng, 6)
    for dim, blocks in cuts:
        draws = jnp.exp(jax.random.uniform(jax.random.fold_in(own, dim), (blocks,), jnp.float32, smallest / len(cuts), high / len(cuts)))
        factor_of = factor_of * jnp.repeat(draws, extent[dim] // blocks).reshape([-1 if axis == dim else 1 for axis in range(len(extent))])
    return factor_of


def noise(stream_key, shape, scale, limit, cuts=(), held_as=jnp.bfloat16):
    values = jax.random.normal(stream_key, shape, jnp.float32) * scale
    if len(cuts) > 0:
        values = block_levels(stream_key, shape, cuts, -0.22, 0.18) * values
    return jnp.clip(values, min=-limit, max=limit).astype(held_as)


def setup_inputs(seed: int = 0) -> dict:
    streams_of = jax.random.split(jax.random.key(seed), 11)
    inputs = noise(streams_of[0], (TOKENS, D), 1.0, 6.0, ((0, 16),))
    cotangent = noise(streams_of[1], (TOKENS, D), 1.0, 6.0, ((0, 16),))
    segments = draw_segments(jax.random.fold_in(streams_of[10], 71), 0)
    qkv_weight = noise(streams_of[3], (2, D, 3 * D), D ** -0.5, 0.21875, ((0, 2), (1, 16)))
    out_weight = noise(streams_of[4], (2, D, D), (D // 16) ** -0.5, 0.875, ((0, 2), (1, 16)))
    up_weight = noise(streams_of[5], (2, D, FF), D ** -0.5, 0.21875, ((0, 2), (1, 16)))
    down_weight = noise(streams_of[6], (2, FF, D), FF ** -0.5, 0.109375, ((0, 2), (1, 16)))
    norm_params = jnp.clip(0.5 + 1.0 * jax.random.uniform(streams_of[7], (2, 4, D), jnp.float32) ** block_levels(streams_of[7], (2, 4, D), ((0, 2), (2, 16)), -0.2, 0.2), 0.5, 1.5).astype(jnp.bfloat16)
    bias_params = noise(streams_of[8], (2, 4, D), 0.5, 3.0, ((0, 2), (2, 16)))
    up_bias = noise(streams_of[9], (2, FF), 0.5, 3.0, ((0, 2), (1, 16)))
    return dict(inputs=inputs, cotangent=cotangent, segments=segments, qkv_weight=qkv_weight, out_weight=out_weight, up_weight=up_weight, down_weight=down_weight, norm_params=norm_params, bias_params=bias_params, up_bias=up_bias)


EPS = 1e-05
HALF_ROOT = 0.7071067811865476
INV_ROOT_TAU = 0.3989422804014327
NEGATIVE = -1e+30

def mix(form, left, right):
    return jnp.einsum(form, left.astype(jnp.float32), right.astype(jnp.float32))

def layer_normalize(input_float, norm_gain, norm_shift):
    row_mean = lax.optimization_barrier(jnp.mean(input_float, axis=-1, keepdims=True))
    centered_input = input_float - row_mean
    inverse_deviation = lax.rsqrt(lax.optimization_barrier(jnp.mean(centered_input * centered_input, axis=-1, keepdims=True)) + EPS)
    standardized_input = centered_input * inverse_deviation
    return (standardized_input, inverse_deviation, (standardized_input * norm_gain + norm_shift).astype(jnp.bfloat16))

def layer_normalize_backward(normed_gradient, standardized_input, inverse_deviation, norm_gain):
    standardized_gradient = normed_gradient * norm_gain
    inner_width = lax.optimization_barrier(jnp.mean(standardized_gradient, axis=-1, keepdims=True)) + standardized_input * lax.optimization_barrier(jnp.mean(standardized_gradient * standardized_input, axis=-1, keepdims=True))
    return (inverse_deviation * (standardized_gradient - inner_width), lax.optimization_barrier(jnp.sum(normed_gradient * standardized_input, axis=0)), lax.optimization_barrier(jnp.sum(normed_gradient, axis=0)))

def rotary_tables(seg):
    width = seg.shape[1]
    index = jnp.broadcast_to(jnp.arange(width, dtype=jnp.int32)[None, :], seg.shape)
    before = jnp.concatenate([seg[:, :1] - 1, seg[:, :-1]], axis=1)
    first = lax.cummax(jnp.where(seg != before, index, 0), axis=1)
    place = (index - first).astype(jnp.float32)
    freq = 10000.0 ** (-jnp.arange(0, ROT, 2, dtype=jnp.float32) / ROT)
    angle = place[:, :, None, None] * freq
    return (jnp.cos(angle), jnp.sin(angle))

def rotate(tensor, cosine, sine, sign):
    half = ROT // 2
    first = tensor[..., :half]
    second = tensor[..., half:ROT]
    return jnp.concatenate([first * cosine - sign * second * sine, second * cosine + sign * first * sine, tensor[..., ROT:]], axis=-1)

def scores(query_rows, key_rows, seg):
    width = seg.shape[1]
    raw = mix('prhe,pshe->phrs', query_rows, key_rows) * (1.0 / math.sqrt(HEAD))
    index = jnp.arange(width, dtype=jnp.int32)
    causal = index[:, None] >= index[None, :]
    allowed = (seg[:, None, :, None] == seg[:, None, None, :]) & causal[None, None]
    return jnp.where(allowed, raw, NEGATIVE)

def forward(x, seg, weights):
    wqkv, wout, wup, wdown, norm_pairs, abias, upbias = weights
    packs, width = seg.shape
    shape = (packs, width, D // HEAD, HEAD)
    norm_pairs = norm_pairs.astype(jnp.float32)
    abias = abias.astype(jnp.float32)
    upbias = upbias.astype(jnp.float32)
    input_float = x.astype(jnp.float32)
    first_standardized, first_inverse_deviation, first_normed = layer_normalize(input_float, norm_pairs[0], norm_pairs[1])
    second_standardized, second_inverse_deviation, second_normed = layer_normalize(input_float, norm_pairs[2], norm_pairs[3])
    qkv = jnp.dot(first_normed, wqkv, preferred_element_type=jnp.float32)
    cosine, sine = rotary_tables(seg)
    query_rows = rotate((qkv[:, :D] + abias[0]).reshape(shape), cosine, sine, 1.0).astype(jnp.bfloat16)
    key_rows = rotate(qkv[:, D:2 * D].reshape(shape), cosine, sine, 1.0).astype(jnp.bfloat16)
    value_rows = (qkv[:, 2 * D:] + abias[1]).reshape(shape).astype(jnp.bfloat16)
    raw = scores(query_rows, key_rows, seg)
    top = lax.optimization_barrier(jnp.max(raw, axis=-1, keepdims=True))
    log_sum_exp = top + jnp.log(lax.optimization_barrier(jnp.sum(jnp.exp(raw - top), axis=-1, keepdims=True)))
    probs = jnp.exp(raw - log_sum_exp).astype(jnp.bfloat16)
    context_rows = mix('phrs,pshe->prhe', probs, value_rows).reshape(packs * width, D).astype(jnp.bfloat16)
    attended = jnp.dot(context_rows, wout, preferred_element_type=jnp.float32) + abias[2]
    hidden_rows = jnp.dot(second_normed, wup, preferred_element_type=jnp.float32) + upbias
    activation_output = (0.5 * hidden_rows * (1.0 + lax.erf(hidden_rows * HALF_ROOT))).astype(jnp.bfloat16)
    mlp = jnp.dot(activation_output, wdown, preferred_element_type=jnp.float32) + abias[3]
    result = (input_float + attended + mlp).astype(jnp.bfloat16)
    saved_state = (first_standardized, first_inverse_deviation, first_normed, second_standardized, second_inverse_deviation, second_normed, query_rows, key_rows, value_rows, log_sum_exp, context_rows, hidden_rows, activation_output)
    return (result, saved_state)

def backward(saved_state, upstream, seg, weights):
    wqkv, wout, wup, wdown, norm_pairs, abias, upbias = weights
    first_standardized, first_inverse_deviation, first_normed, second_standardized, second_inverse_deviation, second_normed, query_rows, key_rows, value_rows, log_sum_exp, context_rows, hidden_rows, activation_output = saved_state
    packs, width = seg.shape
    shape = (packs, width, D // HEAD, HEAD)
    norm_pairs = norm_pairs.astype(jnp.float32)
    upf = upstream.astype(jnp.float32)
    d_down = jnp.dot(activation_output.T, upstream, preferred_element_type=jnp.float32)
    dgelu = jnp.dot(upstream, wdown.T, preferred_element_type=jnp.float32)
    slope = 0.5 * (1.0 + lax.erf(hidden_rows * HALF_ROOT)) + hidden_rows * INV_ROOT_TAU * jnp.exp(-0.5 * hidden_rows * hidden_rows)
    dhidden = dgelu * slope
    dhidden_low = dhidden.astype(jnp.bfloat16)
    d_up = jnp.dot(second_normed.T, dhidden_low, preferred_element_type=jnp.float32)
    second_norm_gradient = jnp.dot(dhidden_low, wup.T, preferred_element_type=jnp.float32)
    d_out = jnp.dot(context_rows.T, upstream, preferred_element_type=jnp.float32)
    dctx = jnp.dot(upstream, wout.T, preferred_element_type=jnp.float32).reshape(shape).astype(jnp.bfloat16)
    probs = jnp.exp(scores(query_rows, key_rows, seg) - log_sum_exp)
    dvalues = mix('phrs,prhe->pshe', probs.astype(jnp.bfloat16), dctx)
    dprobs = mix('prhe,pshe->phrs', dctx, value_rows)
    dscores = (probs * (dprobs - lax.optimization_barrier(jnp.sum(probs * dprobs, axis=-1, keepdims=True))) * (1.0 / math.sqrt(HEAD))).astype(jnp.bfloat16)
    dquery = mix('phrs,pshe->prhe', dscores, key_rows)
    dkeys = mix('phrs,prhe->pshe', dscores, query_rows)
    cosine, sine = rotary_tables(seg)
    dquery = rotate(dquery, cosine, sine, -1.0).reshape(packs * width, D)
    dkeys = rotate(dkeys, cosine, sine, -1.0).reshape(packs * width, D)
    dvalues = dvalues.reshape(packs * width, D)
    dqkv = jnp.concatenate([dquery, dkeys, dvalues], axis=1).astype(jnp.bfloat16)
    d_qkv = jnp.dot(first_normed.T, dqkv, preferred_element_type=jnp.float32)
    first_norm_gradient = jnp.dot(dqkv, wqkv.T, preferred_element_type=jnp.float32)
    first_input_gradient, first_gain_gradient, first_shift_gradient = layer_normalize_backward(first_norm_gradient, first_standardized, first_inverse_deviation, norm_pairs[0])
    second_input_gradient, second_gain_gradient, second_shift_gradient = layer_normalize_backward(second_norm_gradient, second_standardized, second_inverse_deviation, norm_pairs[2])
    grad_in = (upf + first_input_gradient + second_input_gradient).astype(jnp.bfloat16)
    d_norm = jnp.stack([first_gain_gradient, first_shift_gradient, second_gain_gradient, second_shift_gradient])
    column = lax.optimization_barrier(jnp.sum(upf, axis=0))
    d_bias = jnp.stack([lax.optimization_barrier(jnp.sum(dquery, axis=0)), lax.optimization_barrier(jnp.sum(dvalues, axis=0)), column, column])
    d_upbias = lax.optimization_barrier(jnp.sum(dhidden, axis=0))
    return (grad_in, (d_qkv, d_out, d_up, d_down, d_norm, d_bias, d_upbias))

def reference(inputs, cotangent, segments, qkv_weight, out_weight, up_weight, down_weight, norm_params, bias_params, up_bias):
    packs = TOKENS // PACK
    group = 32 if packs % 32 == 0 else packs
    blocks = packs // group
    seg_all = segments.reshape(blocks, group, PACK)
    x_all = inputs.reshape(blocks, group * PACK, D)
    c_all = cotangent.reshape(blocks, group * PACK, D)
    params = (qkv_weight, out_weight, up_weight, down_weight, norm_params, bias_params, up_bias)

    def select_layer(level):
        return tuple((piece[level] for piece in params))

    def one_block(carry, item):
        xin, cot, seg = item
        first_out, first_saved = forward(xin, seg, select_layer(0))
        second_out, second_saved = forward(first_out, seg, select_layer(1))
        middle_grad, second_grads = backward(second_saved, cot, seg, select_layer(1))
        input_grad, first_grads = backward(first_saved, middle_grad, seg, select_layer(0))
        total = tuple((acc + jnp.stack([left, right]) for acc, left, right in zip(carry, first_grads, second_grads)))
        return (total, (jnp.stack([first_out, second_out]), jnp.stack([input_grad, middle_grad])))
    init = tuple((jnp.zeros(piece.shape, jnp.float32) for piece in params))
    total, (outs, grads_in) = lax.scan(one_block, init, (x_all, c_all, seg_all))
    outs = jnp.transpose(outs, (1, 0, 2, 3)).reshape(2, TOKENS, D)
    grads_in = jnp.transpose(grads_in, (1, 0, 2, 3)).reshape(2, TOKENS, D)
    return (outs, grads_in, total[0], total[1], total[2], total[3], total[4], total[5], total[6])
```

```python
import math

import jax
import jax.numpy as jnp
from jax import lax
from jax.sharding import PartitionSpec as P

D = 768
FF = 3072
HEAD = 64
ROT = 16
PACK = 128
LANES = 128


EPS = 1e-05
HALF_ROOT = 0.7071067811865476
INV_ROOT_TAU = 0.3989422804014327
NEGATIVE = -1e30


def shifted(value, axis, steps):
    count = lax.axis_size(axis)
    initial, last = (max(0, -steps), min(count, count - steps))
    return lax.ppermute(value, axis, [(source, source + steps) for source in range(initial, last)])


def mix(form, left, right):
    return jnp.einsum(form, left, right, preferred_element_type=jnp.float32)


def layer_normalize(input_float, norm_gain, norm_shift):
    row_mean = jnp.mean(input_float, axis=-1, keepdims=True)
    centered_input = input_float - row_mean
    inverse_deviation = lax.rsqrt(
        jnp.mean(centered_input * centered_input, axis=-1, keepdims=True) + EPS
    )
    standardized_input = centered_input * inverse_deviation
    return (
        standardized_input,
        inverse_deviation,
        (standardized_input * norm_gain + norm_shift).astype(jnp.bfloat16),
    )


def layer_normalize_backward(normed_gradient, standardized_input, inverse_deviation, norm_gain):
    standardized_gradient = normed_gradient * norm_gain
    inner_width = jnp.mean(
        standardized_gradient, axis=-1, keepdims=True
    ) + standardized_input * jnp.mean(
        standardized_gradient * standardized_input, axis=-1, keepdims=True
    )
    return (
        inverse_deviation * (standardized_gradient - inner_width),
        jnp.sum(normed_gradient * standardized_input, axis=0),
        jnp.sum(normed_gradient, axis=0),
    )


def rotary_tables(seg):
    width = seg.shape[1]
    index = jnp.arange(width, dtype=jnp.int32)[None, :]
    before = jnp.concatenate([seg[:, :1] - 1, seg[:, :-1]], axis=1)
    first = lax.cummax(jnp.where(seg != before, index, 0), axis=1)
    place = (index - first).astype(jnp.float32)
    freq = 10000.0 ** (-jnp.arange(0, ROT, 2, dtype=jnp.float32) / ROT)
    angle = place[:, :, None, None] * freq
    return (jnp.cos(angle), jnp.sin(angle))


def rotate(tensor, cosine, sine, sign):
    half = ROT // 2
    first = tensor[..., :half]
    second = tensor[..., half:ROT]
    return jnp.concatenate(
        [
            first * cosine - sign * second * sine,
            second * cosine + sign * first * sine,
            tensor[..., ROT:],
        ],
        axis=-1,
    )


def scores(query_rows, key_rows, seg):
    width = seg.shape[1]
    raw = mix("prhe,pshe->phrs", query_rows, key_rows) * (1.0 / math.sqrt(HEAD))
    index = jnp.arange(width, dtype=jnp.int32)
    causal = index[:, None] >= index[None, :]
    allowed = (seg[:, None, :, None] == seg[:, None, None, :]) & causal[None, None]
    return jnp.where(allowed, raw, NEGATIVE)


def forward(x, seg, weights):
    wqkv, wout, wup, wdown, norm_pairs, abias, upbias = weights
    packs, width = seg.shape
    shape = (packs, width, D // HEAD, HEAD)
    norm_pairs = norm_pairs.astype(jnp.float32)
    abias = abias.astype(jnp.float32)
    upbias = upbias.astype(jnp.float32)
    input_float = x.astype(jnp.float32)
    first_standardized, first_inverse_deviation, first_normed = layer_normalize(
        input_float, norm_pairs[0], norm_pairs[1]
    )
    second_standardized, second_inverse_deviation, second_normed = layer_normalize(
        input_float, norm_pairs[2], norm_pairs[3]
    )
    qkv = jnp.dot(first_normed, wqkv, preferred_element_type=jnp.float32)
    cosine, sine = rotary_tables(seg)
    query_rows = rotate((qkv[:, :D] + abias[0]).reshape(shape), cosine, sine, 1.0).astype(
        jnp.bfloat16
    )
    key_rows = rotate(qkv[:, D : 2 * D].reshape(shape), cosine, sine, 1.0).astype(jnp.bfloat16)
    value_rows = (qkv[:, 2 * D :] + abias[1]).reshape(shape).astype(jnp.bfloat16)
    raw = scores(query_rows, key_rows, seg)
    top = jnp.max(raw, axis=-1, keepdims=True)
    log_sum_exp = top + jnp.log(jnp.sum(jnp.exp(raw - top), axis=-1, keepdims=True))
    probs = jnp.exp(raw - log_sum_exp).astype(jnp.bfloat16)
    context_rows = (
        mix("phrs,pshe->prhe", probs, value_rows).reshape(packs * width, D).astype(jnp.bfloat16)
    )
    attended = jnp.dot(context_rows, wout, preferred_element_type=jnp.float32) + abias[2]
    hidden_rows = jnp.dot(second_normed, wup, preferred_element_type=jnp.float32) + upbias
    activation_output = (0.5 * hidden_rows * (1.0 + lax.erf(hidden_rows * HALF_ROOT))).astype(
        jnp.bfloat16
    )
    mlp = jnp.dot(activation_output, wdown, preferred_element_type=jnp.float32) + abias[3]
    result = (input_float + attended + mlp).astype(jnp.bfloat16)
    saved_state = (
        first_standardized,
        first_inverse_deviation,
        first_normed,
        second_standardized,
        second_inverse_deviation,
        second_normed,
        query_rows,
        key_rows,
        value_rows,
        log_sum_exp,
        context_rows,
        hidden_rows,
        activation_output,
    )
    return (result, saved_state)


def backward(saved_state, upstream, seg, weights):
    wqkv, wout, wup, wdown, norm_pairs, abias, upbias = weights
    (
        first_standardized,
        first_inverse_deviation,
        first_normed,
        second_standardized,
        second_inverse_deviation,
        second_normed,
        query_rows,
        key_rows,
        value_rows,
        log_sum_exp,
        context_rows,
        hidden_rows,
        activation_output,
    ) = saved_state
    packs, width = seg.shape
    shape = (packs, width, D // HEAD, HEAD)
    norm_pairs = norm_pairs.astype(jnp.float32)
    upf = upstream.astype(jnp.float32)
    d_down = jnp.dot(activation_output.T, upstream, preferred_element_type=jnp.float32).astype(
        jnp.bfloat16
    )
    dgelu = jnp.dot(upstream, wdown.T, preferred_element_type=jnp.float32)
    slope = 0.5 * (1.0 + lax.erf(hidden_rows * HALF_ROOT)) + hidden_rows * INV_ROOT_TAU * jnp.exp(
        -0.5 * hidden_rows * hidden_rows
    )
    dhidden = dgelu * slope
    dhidden_low = dhidden.astype(jnp.bfloat16)
    d_up = jnp.dot(second_normed.T, dhidden_low, preferred_element_type=jnp.float32)
    second_norm_gradient = jnp.dot(dhidden_low, wup.T, preferred_element_type=jnp.float32)
    d_out = jnp.dot(context_rows.T, upstream, preferred_element_type=jnp.float32)
    dctx = (
        jnp.dot(upstream, wout.T, preferred_element_type=jnp.float32)
        .reshape(shape)
        .astype(jnp.bfloat16)
    )
    probs = jnp.exp(scores(query_rows, key_rows, seg) - log_sum_exp)
    dvalues = mix("phrs,prhe->pshe", probs.astype(jnp.bfloat16), dctx)
    dprobs = mix("prhe,pshe->phrs", dctx, value_rows)
    dscores = (
        probs * (dprobs - jnp.sum(probs * dprobs, axis=-1, keepdims=True)) * (1.0 / math.sqrt(HEAD))
    ).astype(jnp.bfloat16)
    dquery = mix("phrs,pshe->prhe", dscores, key_rows)
    dkeys = mix("phrs,prhe->pshe", dscores, query_rows)
    cosine, sine = rotary_tables(seg)
    dquery = rotate(dquery, cosine, sine, -1.0).reshape(packs * width, D)
    dkeys = rotate(dkeys, cosine, sine, -1.0).reshape(packs * width, D)
    dvalues = dvalues.reshape(packs * width, D)
    dqkv = jnp.concatenate([dquery, dkeys, dvalues], axis=1).astype(jnp.bfloat16)
    d_qkv = jnp.dot(first_normed.T, dqkv, preferred_element_type=jnp.float32)
    first_norm_gradient = jnp.dot(dqkv, wqkv.T, preferred_element_type=jnp.float32)
    first_input_gradient, first_gain_gradient, first_shift_gradient = layer_normalize_backward(
        first_norm_gradient, first_standardized, first_inverse_deviation, norm_pairs[0]
    )
    second_input_gradient, second_gain_gradient, second_shift_gradient = layer_normalize_backward(
        second_norm_gradient, second_standardized, second_inverse_deviation, norm_pairs[2]
    )
    grad_in = (upf + first_input_gradient + second_input_gradient).astype(jnp.bfloat16)
    d_norm = jnp.stack(
        [first_gain_gradient, first_shift_gradient, second_gain_gradient, second_shift_gradient]
    )
    column = jnp.sum(upf, axis=0)
    d_bias = jnp.stack([jnp.sum(dquery, axis=0), jnp.sum(dvalues, axis=0), column, column])
    d_upbias = jnp.sum(dhidden, axis=0)
    return (grad_in, (d_qkv, d_out, d_up, d_down, d_norm, d_bias, d_upbias))


def send_forward(result):
    return shifted(result, "section", 1)


def send_back(grad_in):
    return shifted(grad_in, "section", -1)


def on_device(
    inputs,
    cotangent,
    segments,
    qkv_weight,
    out_weight,
    up_weight,
    down_weight,
    norm_params,
    bias_params,
    up_bias,
):
    is_first = lax.axis_index("section") == 0
    rows = qkv_weight.shape[1]
    tokens = inputs.shape[0]
    seg = segments.reshape(tokens // PACK, PACK)

    small = jnp.concatenate(
        [norm_params[0].T, bias_params[0].T, up_bias.reshape(rows, FF // D)], axis=1
    )
    small_width = small.shape[1]
    small = jnp.pad(small, ((0, 0), (0, LANES - small_width)))
    packed = jnp.concatenate([small, qkv_weight[0], out_weight[0], up_weight[0]], axis=1)
    cuts = [LANES, LANES + 3 * D, LANES + 4 * D]
    packed = lax.all_gather(packed, "dp", axis=0, tiled=True)
    wdown = lax.all_gather(down_weight[0], "dp", axis=0, tiled=True)
    small, wqkv, wout, wup = jnp.split(packed, cuts, axis=1)
    small = small[:, :small_width].T
    weights = (wqkv, wout, wup, wdown, small[:4], small[4:8], small[8:].T.reshape(FF))

    lead, _ = forward(inputs, seg, weights)
    x = jnp.where(is_first, inputs, send_forward(lead))
    layer_out, saved_state = forward(x, seg, weights)
    trail, _ = backward(saved_state, cotangent, seg, weights)
    upstream = jnp.where(is_first, send_back(trail), cotangent)
    input_grad, grads = backward(saved_state, upstream, seg, weights)
    d_qkv, d_out, d_up, d_down, d_norm, d_bias, d_upbias = grads

    d_down = lax.psum_scatter(d_down, "dp", scatter_dimension=0, tiled=True)
    d_small = jnp.concatenate([d_norm.T, d_bias.T, d_upbias.reshape(D, FF // D)], axis=1)
    d_small = jnp.pad(d_small, ((0, 0), (0, LANES - small_width)))
    owned = jnp.concatenate(
        [piece.astype(jnp.bfloat16) for piece in (d_small, d_qkv, d_out, d_up)], axis=1
    )
    owned = lax.psum_scatter(owned, "dp", scatter_dimension=0, tiled=True).astype(jnp.float32)
    d_small, d_qkv, d_out, d_up = jnp.split(owned, cuts, axis=1)
    return (
        layer_out[None],
        input_grad[None],
        d_qkv[None],
        d_out[None],
        d_up[None],
        d_down.astype(jnp.float32)[None],
        d_small[:, :4].T[None],
        d_small[:, 4:8].T[None],
        d_small[:, 8:small_width].reshape(1, -1),
    )


def solution(mesh):
    in_specs = (
        P("dp", None),
        P("dp", None),
        P("dp"),
        P("section", "dp", None),
        P("section", "dp", None),
        P("section", "dp", None),
        P("section", "dp", None),
        P("section", None, "dp"),
        P("section", None, "dp"),
        P("section", "dp"),
    )
    out_specs = (
        P("section", "dp", None),
        P("section", "dp", None),
        P("section", "dp", None),
        P("section", "dp", None),
        P("section", "dp", None),
        P("section", "dp", None),
        P("section", None, "dp"),
        P("section", None, "dp"),
        P("section", "dp"),
    )
    return jax.shard_map(
        on_device, mesh=mesh, in_specs=in_specs, out_specs=out_specs, check_vma=False
    )
```
